32 devices in a mesh: grp: 2 (over x), sub: 16 (over z, y, core).
Axes of the slice: x: 2, y: 2, z: 4, core: 2. Of those that a mesh axis runs over, the one named last changes fastest.
Arguments:
- load_cases: float32 [36864, 128], P(('grp', 'sub')), may hold values from -6 to 6
- schur_matrix: float32 [36864, 1152], P(('grp', 'sub')), may hold values from -0.0017361111 to 16, as said below
- local_inverse: float32 [36864, 1152], P(('grp', 'sub')), may hold values from -0.00021701389 to 2, as said below
- coarse_basis: float32 [1024, 1152], P(('grp', 'sub')), may hold values from -0.375 to 0.375
- group_inverse: float32 [1024, 512], P(('grp', 'sub')), may hold values from -0.0009765625 to 4, as said below
- group_modes: float32 [1024, 32], P(('grp', 'sub')), may hold values from -0.375 to 0.375
- top_inverse: float32 [64, 64], replicated, may hold values from -0.0078125 to 4, as said below
- face_map: int32 [32, 1152], P(('grp', 'sub')), may hold values from 0 to 1151, each once within a row
- spectrum: float32 [2], replicated, may hold values from 0.1 to 6, as said below
Outputs:
- solution: float32 [36864, 128], P(('grp', 'sub'))
- residual: float32 [36864, 128], P(('grp', 'sub'))
The draws below stay inside these ranges and needn't reach their ends.
Inputs may be any that keep to these rules, and one draw needn't show every extreme that they name: `face_map`: each row is a permutation of 0 to 1151. `schur_matrix`: each subdomain's 1152 x 1152 block is symmetric positive definite. `local_inverse`: each subdomain's 1152 x 1152 block is symmetric positive definite. `group_inverse`: each group's 512 x 512 block is symmetric positive definite. `top_inverse`: symmetric positive definite. spectrum[0] < spectrum[1].
All inputs are finite; a program needn't handle non-finite values.
Results may differ from the reference program's by a relative error of at most 0.00011.
Values sent between devices are 32-bit elements; how exact they have to be, the bound alone decides.
A program may use at most 64 MiB of HBM per device.

```python
import math
import jax
import jax.numpy as jnp
from jax import lax

FACE = 288
ORDER = 1152
MODES = 32
CASES = 128
ITERS = 3
DOMAINS = 32
COARSE = 512
APEX_DOFS = 64
N_GRP = 2
N_SUB = 16


def dominant(key, number, order, spread, diag_low, diag_high):
    first_key, second_key = jax.random.split(key)
    raw = jax.random.uniform(first_key, (number, order, order), jnp.float32, -1.0, 1.0)
    offdiag = (raw + jnp.swapaxes(raw, 1, 2)) * (0.5 * spread / order)
    levels = jnp.exp(jax.random.uniform(second_key, (number, order, 1), jnp.float32, math.log(diag_low), math.log(diag_high)))
    diagonal_mask = lax.broadcasted_iota(jnp.int32, (order, order), 0) == lax.broadcasted_iota(jnp.int32, (order, order), 1)
    return jnp.where(diagonal_mask[None], levels, offdiag)


def draw_schur_matrix(key, part):
    blocks = dominant(key, DOMAINS, ORDER, 2.0, 2.0, 4.0)
    return blocks.reshape(DOMAINS * ORDER, ORDER)


def draw_local_inverse(key, part):
    blocks = dominant(key, DOMAINS, ORDER, 0.25, 0.25, 0.5)
    return blocks.reshape(DOMAINS * ORDER, ORDER)


def draw_group_inverse(key, part):
    groups = APEX_DOFS // MODES
    blocks = dominant(key, groups, COARSE, 0.5, 0.5, 1.0)
    return blocks.reshape(groups * COARSE, COARSE)


def draw_top_inverse(key, part):
    blocks = dominant(key, 1, APEX_DOFS, 0.5, 0.5, 1.0)
    return blocks[0]


def draw_spectrum(key, part):
    first_key, second_key = jax.random.split(key)
    lower = jax.random.uniform(first_key, (), jnp.float32, 0.2, 0.4)
    upper = jax.random.uniform(second_key, (), jnp.float32, 2.5, 4.0)
    return jnp.stack([lower, upper])


def shard_levels(stream_key, shape, cuts, low, top_value):
    loudness, own = 1.0, jax.random.fold_in(stream_key, 6)
    for dim, parts in cuts:
        draws = jnp.exp(jax.random.uniform(jax.random.fold_in(own, dim), (parts,), jnp.float32, low / len(cuts), top_value / len(cuts)))
        loudness = loudness * jnp.repeat(draws, shape[dim] // parts).reshape([-1 if axis == dim else 1 for axis in range(len(shape))])
    return loudness


def normal_values(rng, dims, deviation, limit, shards=(), held_as=jnp.bfloat16):
    level = shard_levels(rng, dims, shards, -0.22, 0.18) if shards else 1.0
    values = jax.random.normal(rng, dims, jnp.float32) * deviation * level
    return jnp.minimum(jnp.maximum(values, -limit), limit).astype(held_as)


def setup_inputs(seed: int = 0) -> dict:
    key_of = jax.random.split(jax.random.key(seed), 10)
    load_cases = normal_values(key_of[0], (DOMAINS * ORDER, CASES), 1.0, 6.0, ((0, 32),), jnp.float32)
    schur_matrix = draw_schur_matrix(jax.random.fold_in(key_of[9], 71), 0)
    local_inverse = draw_local_inverse(jax.random.fold_in(key_of[9], 71), 0)
    coarse_basis = normal_values(key_of[3], (DOMAINS * MODES, ORDER), (ORDER // 4) ** -0.5, 0.375, ((0, 32),), jnp.float32)
    group_inverse = draw_group_inverse(jax.random.fold_in(key_of[9], 71), 0)
    group_modes = normal_values(key_of[5], (DOMAINS * MODES, MODES), (8 * MODES) ** -0.5, 0.375, ((0, 32),), jnp.float32)
    top_inverse = draw_top_inverse(jax.random.fold_in(key_of[9], 71), 0)
    face_map = jax.vmap(lambda own: jax.random.permutation(own, ORDER))(jax.random.split(key_of[7], DOMAINS)).reshape((DOMAINS, ORDER)).astype(jnp.int32)
    spectrum = draw_spectrum(jax.random.fold_in(key_of[9], 71), 0)
    return dict(load_cases=load_cases, schur_matrix=schur_matrix, local_inverse=local_inverse, coarse_basis=coarse_basis, group_inverse=group_inverse, group_modes=group_modes, top_inverse=top_inverse, face_map=face_map, spectrum=spectrum)


def assemble(values, face_map, inverse_map):
    columns = values.shape[-1]
    face_rows = jnp.take_along_axis(values, face_map[:, :, None], axis=1).reshape(N_GRP, N_SUB, 4, FACE, columns)
    zero_grp = jnp.zeros_like(face_rows[:1, :, 0])
    zero_sub = jnp.zeros_like(face_rows[:, :1, 0])
    from_low = jnp.concatenate([zero_grp, face_rows[:-1, :, 1]], axis=0)
    from_high = jnp.concatenate([face_rows[1:, :, 0], zero_grp], axis=0)
    from_left = jnp.concatenate([zero_sub, face_rows[:, :-1, 3]], axis=1)
    from_right = jnp.concatenate([face_rows[:, 1:, 2], zero_sub], axis=1)
    received = jnp.stack([from_low, from_high, from_left, from_right], axis=2).reshape(DOMAINS, ORDER, columns)
    return values + jnp.take_along_axis(received, inverse_map[:, :, None], axis=1)


def reference(load_cases, schur_matrix, local_inverse, coarse_basis, group_inverse, group_modes, top_inverse, face_map, spectrum):
    largest_bound = lax.Precision.HIGHEST
    inverse_map = jnp.argsort(face_map, axis=1).astype(jnp.int32)
    grp_ids = jnp.arange(N_GRP)[:, None]
    sub_ids = jnp.arange(N_SUB)[None, :]
    has_side = jnp.stack([jnp.broadcast_to(grp_ids > 0, (N_GRP, N_SUB)),
                          jnp.broadcast_to(grp_ids < N_GRP - 1, (N_GRP, N_SUB)),
                          jnp.broadcast_to(sub_ids > 0, (N_GRP, N_SUB)),
                          jnp.broadcast_to(sub_ids < N_SUB - 1, (N_GRP, N_SUB))], axis=-1)
    face_weight = jnp.where(has_side, 0.5, 1.0).astype(jnp.float32).reshape(DOMAINS, 4)
    face_weight = jnp.repeat(face_weight, FACE, axis=1)
    weight = jnp.take_along_axis(face_weight, inverse_map, axis=1)[:, :, None]

    schur_blocks = schur_matrix.reshape(DOMAINS, ORDER, ORDER)
    inverse_blocks = local_inverse.reshape(DOMAINS, ORDER, ORDER)
    basis = coarse_basis.reshape(DOMAINS, MODES, ORDER)
    group_blocks = group_inverse.reshape(N_GRP, COARSE, COARSE)
    cluster_basis = group_modes.reshape(N_GRP, COARSE, MODES)

    def precondition(residual):
        weighted = weight * residual
        local_part = jnp.einsum('dab,dbr->dar', inverse_blocks, weighted, precision=largest_bound)
        coarse = jnp.einsum('dma,dar->dmr', basis, weighted, precision=largest_bound)
        piled_vectors = coarse.reshape(N_GRP, COARSE, -1)
        cluster_portion = jnp.einsum('gab,gbr->gar', group_blocks, piled_vectors, precision=largest_bound)
        apex_input = jnp.einsum('kli,klp->kip', cluster_basis, piled_vectors, precision=largest_bound).reshape(APEX_DOFS, -1)
        apex_output = jnp.dot(top_inverse, apex_input, precision=largest_bound).reshape(N_GRP, MODES, -1)
        update_term = cluster_portion + jnp.einsum('usl,ule->use', cluster_basis, apex_output, precision=largest_bound)
        update_term = update_term.reshape(DOMAINS, MODES, -1)
        summed = local_part + jnp.einsum('dma,dmr->dar', basis, update_term, precision=largest_bound)
        return assemble(weight * summed, face_map, inverse_map)

    centre = 0.5 * (spectrum[0] + spectrum[1])
    half_width = 0.5 * (spectrum[1] - spectrum[0])
    residual = assemble(load_cases.reshape(DOMAINS, ORDER, CASES), face_map, inverse_map)
    direction = precondition(residual) / centre
    rho_now = half_width / centre
    solution = jnp.zeros_like(residual)
    for turn_index in range(ITERS):
        solution = solution + direction
        applied = jnp.einsum('dab,dbr->dar', schur_blocks, direction, precision=largest_bound)
        residual = residual - assemble(applied, face_map, inverse_map)
        if turn_index + 1 < ITERS:
            rho_next = 1.0 / (2.0 * centre / half_width - rho_now)
            direction = rho_next * rho_now * direction + (2.0 * rho_next / half_width) * precondition(residual)
            rho_now = rho_next
    return solution.reshape(DOMAINS * ORDER, CASES), residual.reshape(DOMAINS * ORDER, CASES)
```

```python
import functools

import jax
import jax.numpy as jnp
from jax import lax
from jax.experimental import pallas as pl
from jax.experimental.pallas import tpu as pltpu
from jax.sharding import PartitionSpec as P

ITERS = 3
F32 = jnp.float32
BF16 = jnp.bfloat16
MESH = pl.DeviceIdType.MESH


def dot(a, b):
    return jnp.dot(a, b, preferred_element_type=F32)


def exact_dot(a, b):
    return jnp.dot(a, b, precision=lax.Precision.HIGHEST, preferred_element_type=F32)


def split(v):
    high = v.astype(BF16)
    low = (v - high.astype(F32)).astype(BF16)
    return high, low


def kernel(
    n_grp, n_sub, n_low,
    load, schur, linv, basis, ginv, gm, top, fmap, spec,
    sol_out, res_out,
    stage_a, stage_s, a2, s2, perm, perm_t, b2, x2, xl2, zx2, direction, residual,
    sendb, recvb, cbuf, ubuf, qt, nmat,
    load_sem, face_send, face_recv, hi_send, hi_recv, lo_send, lo_recv, u_send, u_recv,
):
    order, columns = load.shape
    face = order // 4
    modes = basis.shape[0]
    n_high = n_sub // n_low
    g = lax.axis_index("grp")
    j = lax.axis_index("sub")
    high, low = j // n_low, j % n_low
    has = [g > 0, g < n_grp - 1, j > 0, j < n_sub - 1]
    ids = [{"grp": g - 1}, {"grp": g + 1}, {"sub": j - 1}, {"sub": j + 1}]
    weight = [jnp.where(h, 0.5, 1.0).astype(F32) for h in has]

    load_a = pltpu.make_async_copy(linv, stage_a, load_sem.at[0])
    load_s = pltpu.make_async_copy(schur, stage_s, load_sem.at[1])
    load_a.start()
    load_s.start()

    def high_peer(k):
        return lax.rem(high + k, n_high) * n_low + low

    def low_peer(k):
        return high * n_low + lax.rem(low + k, n_low)

    def grp_peer(k):
        return lax.rem(g + k, n_grp)

    barrier = pltpu.get_barrier_semaphore()
    for f in range(4):
        @pl.when(has[f])
        def _():
            pl.semaphore_signal(barrier, inc=1, device_id=ids[f], device_id_type=MESH)
    for k in range(1, n_high):
        pl.semaphore_signal(barrier, inc=1, device_id={"sub": high_peer(k)}, device_id_type=MESH)
    for k in range(1, n_low):
        pl.semaphore_signal(barrier, inc=1, device_id={"sub": low_peer(k)}, device_id_type=MESH)
    for k in range(1, n_grp):
        pl.semaphore_signal(barrier, inc=1, device_id={"grp": grp_peer(k)}, device_id_type=MESH)
    expected = (n_high - 1) + (n_low - 1) + (n_grp - 1)
    for h in has:
        expected = expected + jnp.where(h, 1, 0)
    pl.semaphore_wait(barrier, expected)

    def high_copy(r, k, owner):
        return pltpu.make_async_remote_copy(
            src_ref=cbuf.at[r, owner], dst_ref=cbuf.at[r, owner],
            send_sem=hi_send.at[r, k], recv_sem=hi_recv.at[r, k],
            device_id={"sub": high_peer(k)}, device_id_type=MESH)

    def low_copy(r, k, kh, owner):
        return pltpu.make_async_remote_copy(
            src_ref=cbuf.at[r, owner], dst_ref=cbuf.at[r, owner],
            send_sem=lo_send.at[r, k, kh], recv_sem=lo_recv.at[r, k, kh],
            device_id={"sub": low_peer(k)}, device_id_type=MESH)

    def line_owner(kh):
        return lax.rem(high + n_high - kh, n_high) * n_low + low

    def other_owner(k, kh):
        return lax.rem(high + n_high - kh, n_high) * n_low + lax.rem(low + n_low - k, n_low)

    def gather_start(r):
        for k in range(1, n_high):
            high_copy(r, k, j).start()
        for k in range(1, n_low):
            low_copy(r, k, 0, j).start()

    def gather_relay(r):
        for kh in range(1, n_high):
            high_copy(r, kh, line_owner(kh)).wait_recv()
            for k in range(1, n_low):
                low_copy(r, k, kh, line_owner(kh)).start()

    def gather_finish(r):
        for kh in range(n_high):
            for k in range(1, n_low):
                low_copy(r, k, kh, other_owner(k, kh)).wait_recv()

    def gather_drain(r):
        for k in range(1, n_high):
            high_copy(r, k, j).wait_send()
        for kh in range(n_high):
            for k in range(1, n_low):
                low_copy(r, k, kh, line_owner(kh)).wait_send()

    def u_copy(r, k, owner):
        return pltpu.make_async_remote_copy(
            src_ref=ubuf.at[r, owner], dst_ref=ubuf.at[r, owner],
            send_sem=u_send.at[r, k], recv_sem=u_recv.at[r, k],
            device_id={"grp": grp_peer(k)}, device_id_type=MESH)

    def face_copy(r, f):
        return pltpu.make_async_remote_copy(
            src_ref=sendb.at[r, f], dst_ref=recvb.at[r, f ^ 1],
            send_sem=face_send.at[r, f], recv_sem=face_recv.at[r, f ^ 1],
            device_id=ids[f], device_id_type=MESH)

    def face_wait(r, f):
        pltpu.make_async_remote_copy(
            src_ref=sendb.at[r, f], dst_ref=recvb.at[r, f],
            send_sem=face_send.at[r, f], recv_sem=face_recv.at[r, f],
            device_id=ids[f], device_id_type=MESH).wait_recv()

    def send_faces(r, depth, weighted):
        for f in range(4):
            rows = slice(f * face, (f + 1) * face)
            out = dot(perm[rows, :depth], zx2[:depth, :])
            out = out[:, :columns] + out[:, columns:]
            sendb[r, f] = out * weight[f] if weighted else out

            @pl.when(has[f])
            def _():
                face_copy(r, f).start()

    def receive_face(r, f):
        @pl.when(has[f])
        def _():
            face_wait(r, f)
            sendb_rows = sendb[r, f] + recvb[r, f]
            direct[f] = sendb_rows

        @pl.when(jnp.logical_not(has[f]))
        def _():
            direct[f] = sendb[r, f]

    direct = recvb.at[1 + 2 * ITERS]

    def to_local(total):
        def chunk(i, carry):
            rows = pl.ds(pl.multiple_of(i * face, face), face)
            second = pl.ds(pl.multiple_of(order + i * face, face), face)
            out = dot(perm_t[rows, :], x2[...])
            xl2[rows, :] = out.astype(BF16)
            xl2[second, :] = out.astype(BF16)
            if total is not None:
                total[rows, :] += out[:, :columns] + out[:, columns:]
            return carry
        lax.fori_loop(0, 4, chunk, 0)

    def apply(matrix):
        def chunk(i, carry):
            rows = pl.ds(pl.multiple_of(i * face, face), face)
            out = dot(matrix[rows, :], xl2[...])
            upper, lower = split(out[:, :columns] + out[:, columns:])
            zx2[rows, :columns] = upper
            zx2[rows, columns:] = lower
            return carry
        lax.fori_loop(0, 4, chunk, 0)

    cbuf[0, j] = jnp.zeros((modes, columns), F32)
    cbuf[0, j, :, :modes] = gm[...]
    gather_start(0)

    map_row = fmap[...]
    tile = 128

    def build_t(i, carry):
        rows = pl.ds(pl.multiple_of(i * tile, tile), tile)
        local = lax.broadcasted_iota(jnp.int32, (tile, order), 0) + i * tile
        perm_t[rows, :] = jnp.where(local == map_row, 1.0, 0.0).astype(BF16)
        return carry
    lax.fori_loop(0, order // tile, build_t, 0)
    map_column = jnp.broadcast_to(map_row.astype(F32), (tile, order)).T
    lanes = lax.broadcasted_iota(jnp.int32, (order, tile), 1).astype(F32)
    for t in range(order // tile):
        perm[:, t * tile:(t + 1) * tile] = jnp.where(
            map_column == lanes + float(t * tile), 1.0, 0.0).astype(BF16)

    def split_load(i, carry):
        rows = pl.ds(pl.multiple_of(i * face, face), face)
        upper, lower = split(load[rows, :])
        zx2[rows, :columns] = upper
        zx2[rows, columns:] = lower
        return carry
    lax.fori_loop(0, 4, split_load, 0)
    send_faces(0, order, False)

    upper, lower = split(basis[...])
    moved = dot(jnp.concatenate([upper, lower], axis=0), perm_t[...])
    b2[...] = moved.astype(BF16)
    tail = perm.shape[1] - order
    padded = jnp.concatenate([moved, jnp.zeros((tail - 2 * modes, order), F32)], axis=0)
    perm[:, order:] = padded.T.astype(BF16)
    zx2[order:, :] = jnp.zeros((tail, 2 * columns), BF16)

    def split_matrix(stage, matrix):
        def chunk(i, carry):
            rows = pl.ds(pl.multiple_of(i * tile, tile), tile)
            upper, lower = split(stage[rows, :])
            matrix[rows, :order] = upper
            matrix[rows, order:] = lower
            return carry
        lax.fori_loop(0, order // tile, chunk, 0)

    load_a.wait()
    split_matrix(stage_a, a2)
    gather_relay(0)
    load_s.wait()
    split_matrix(stage_s, s2)
    gather_finish(0)
    qt[...] = cbuf[0].reshape(n_sub * modes, columns).T[:modes, :]
    nmat[...] = exact_dot(gm[...], top[pl.ds(pl.multiple_of(g * modes, modes), modes), :])

    for f in range(4):
        receive_face(0, f)
        residual[f] = direct[f]

    sol_out[...] = jnp.zeros((order, columns), F32)
    centre = jnp.full((1, columns), 0.5 * (spec[0] + spec[1]), F32)
    half_width = jnp.full((1, columns), 0.5 * (spec[1] - spec[0]), F32)

    def precondition(r, c):
        for f in range(4):
            rows = slice(f * face, (f + 1) * face)
            upper, lower = split(residual[f] * weight[f])
            x2[rows, :columns] = upper
            x2[rows, columns:] = lower
        products = dot(b2[...], x2[...])
        products = products[:, :columns] + products[:, columns:]
        cbuf[c, j] = products[:modes, :] + products[modes:, :]
        gather_start(c)
        to_local(None)
        apply(a2)
        gather_relay(c)
        gather_finish(c)
        stacked = cbuf[c].reshape(n_sub * modes, columns)
        ubuf[c, g] = exact_dot(qt[...], stacked)
        for k in range(1, n_grp):
            u_copy(c, k, g).start()
        update = exact_dot(ginv[...], stacked)
        for k in range(1, n_grp):
            u_copy(c, k, lax.rem(g + n_grp - k, n_grp)).wait_recv()
        update = update + exact_dot(nmat[...], ubuf[c].reshape(n_grp * modes, columns))
        upper, lower = split(update)
        for base in (order, order + modes):
            zx2[base:base + modes, :columns] = upper
            zx2[base:base + modes, columns:] = lower
        send_faces(r, perm.shape[1], True)
        for f in range(4):
            receive_face(r, f)

    precondition(1, 1)
    for f in range(4):
        direction[f] = direct[f] / centre
    rho = half_width / centre
    for turn in range(ITERS):
        for f in range(4):
            rows = slice(f * face, (f + 1) * face)
            upper, lower = split(direction[f])
            x2[rows, :columns] = upper
            x2[rows, columns:] = lower
        to_local(sol_out)
        apply(s2)
        r = 2 + 2 * turn
        send_faces(r, order, False)
        for f in range(4):
            receive_face(r, f)
            residual[f] = residual[f] - direct[f]
        if turn + 1 < ITERS:
            rho_next = 1.0 / (2.0 * centre / half_width - rho)
            precondition(r + 1, 2 + turn)
            for f in range(4):
                direction[f] = rho_next * rho * direction[f] + (2.0 * rho_next / half_width) * direct[f]
            rho = rho_next

    for f in range(4):
        rows = slice(f * face, (f + 1) * face)
        upper, lower = split(residual[f])
        x2[rows, :columns] = upper
        x2[rows, columns:] = lower

    def finish(i, carry):
        rows = pl.ds(pl.multiple_of(i * face, face), face)
        out = dot(perm_t[rows, :], x2[...])
        res_out[rows, :] = out[:, :columns] + out[:, columns:]
        return carry
    lax.fori_loop(0, 4, finish, 0)

    for r in range(1 + 2 * ITERS):
        for f in range(4):
            @pl.when(has[f])
            def _():
                face_copy(r, f).wait_send()
    for c in range(1 + ITERS):
        gather_drain(c)
        if c > 0:
            for k in range(1, n_grp):
                u_copy(c, k, g).wait_send()


def solution(mesh):
    n_grp, n_sub = mesh.shape["grp"], mesh.shape["sub"]
    n_low = 1
    while n_low * n_low < n_sub:
        n_low *= 2
    n_high = n_sub // n_low

    def step(load, schur, linv, basis, ginv, gm, top, fmap, spec):
        order, columns = load.shape
        modes = basis.shape[0]
        face = order // 4
        tail = -(-2 * modes // 128) * 128
        rounds = 1 + ITERS
        faces = 1 + 2 * ITERS
        vmem = pl.BlockSpec(memory_space=pltpu.VMEM)
        hbm = pl.BlockSpec(memory_space=pl.ANY)
        smem = pl.BlockSpec(memory_space=pltpu.SMEM)
        dma = pltpu.SemaphoreType.DMA
        field = jax.ShapeDtypeStruct((order, columns), F32)
        return pl.pallas_call(
            functools.partial(kernel, n_grp, n_sub, n_low),
            out_shape=(field, field),
            in_specs=[vmem, hbm, hbm, vmem, vmem, vmem, vmem, vmem, smem],
            out_specs=(vmem, vmem),
            scratch_shapes=[
                pltpu.VMEM((order, order), F32),
                pltpu.VMEM((order, order), F32),
                pltpu.VMEM((order, 2 * order), BF16),
                pltpu.VMEM((order, 2 * order), BF16),
                pltpu.VMEM((order, order + tail), BF16),
                pltpu.VMEM((order, order), BF16),
                pltpu.VMEM((2 * modes, order), BF16),
                pltpu.VMEM((order, 2 * columns), BF16),
                pltpu.VMEM((2 * order, 2 * columns), BF16),
                pltpu.VMEM((order + tail, 2 * columns), BF16),
                pltpu.VMEM((4, face, columns), F32),
                pltpu.VMEM((4, face, columns), F32),
                pltpu.VMEM((faces, 4, face, columns), F32),
                pltpu.VMEM((faces + 1, 4, face, columns), F32),
                pltpu.VMEM((rounds, n_sub, modes, columns), F32),
                pltpu.VMEM((rounds, n_grp, modes, columns), F32),
                pltpu.VMEM((modes, n_sub * modes), F32),
                pltpu.VMEM((modes, n_grp * modes), F32),
                dma((2,)),
                dma((faces, 4)),
                dma((faces, 4)),
                dma((rounds, n_high)),
                dma((rounds, n_high)),
                dma((rounds, n_low, n_high)),
                dma((rounds, n_low, n_high)),
                dma((rounds, n_grp)),
                dma((rounds, n_grp)),
            ],
            compiler_params=pltpu.CompilerParams(
                collective_id=0, has_side_effects=True, vmem_limit_bytes=60 * 1024 * 1024
            ),
        )(load, schur, linv, basis, ginv, gm, top, fmap, spec)

    row = P(("grp", "sub"), None)
    return jax.shard_map(
        step,
        mesh=mesh,
        in_specs=(row, row, row, row, row, row, P(), row, P()),
        out_specs=(row, row),
        check_vma=False,
    )
```

```python
import functools

import jax
import jax.numpy as jnp
from jax import lax
from jax.experimental import pallas as pl
from jax.experimental.pallas import tpu as pltpu
from jax.sharding import PartitionSpec as P

ITERS = 3
F32 = jnp.float32
BF16 = jnp.bfloat16
MESH = pl.DeviceIdType.MESH


def dot(a, b):
    return jnp.dot(a, b, preferred_element_type=F32)


def exact_dot(a, b):
    return jnp.dot(a, b, precision=lax.Precision.HIGHEST, preferred_element_type=F32)


def split(v):
    high = v.astype(BF16)
    low = (v - high.astype(F32)).astype(BF16)
    return high, low


def kernel(
    n_grp, n_sub, n_low,
    load, schur, linv, basis, ginv, gm, top, fmap, spec,
    sol_out, res_out,
    stage_a, stage_s, a2, s2, sp2, perm, perm_t, b2, x2, xl2, zx2, direction, residual,
    sendb, recvb, line_modes, peer_modes, peer_rows, line, part_out, part_in, ubuf, top_in, rq, nmat,
    load_sem, face_send, face_recv, hi_send, hi_recv, lo_send, lo_recv, k_send, k_recv, u_send, u_recv,
):
    order, columns = load.shape
    face = order // 4
    modes = basis.shape[0]
    n_high = n_sub // n_low
    g = lax.axis_index("grp")
    j = lax.axis_index("sub")
    high, low = j // n_low, j % n_low
    has = [g > 0, g < n_grp - 1, j > 0, j < n_sub - 1]
    ids = [{"grp": g - 1}, {"grp": g + 1}, {"sub": j - 1}, {"sub": j + 1}]
    first = jnp.where(g == 0, 1, 0)
    third = jnp.where(j == 0, 1, 0)
    sequence = [("grp", first), ("grp", 1 - first), ("sub", third), ("sub", 1 - third)]
    weight = [jnp.where(h, 0.5, 1.0).astype(F32) for h in has]

    load_a = pltpu.make_async_copy(linv, stage_a, load_sem.at[0])
    load_s = pltpu.make_async_copy(schur, stage_s, load_sem.at[1])
    load_a.start()
    load_s.start()

    def high_peer(k):
        return lax.rem(high + k, n_high) * n_low + low

    def low_peer(k):
        return high * n_low + lax.rem(low + k, n_low)

    def grp_peer(k):
        return lax.rem(g + k, n_grp)

    barrier = pltpu.get_barrier_semaphore()
    for f in range(4):
        @pl.when(has[f])
        def _():
            pl.semaphore_signal(barrier, inc=1, device_id=ids[f], device_id_type=MESH)
    for k in range(1, n_high):
        pl.semaphore_signal(barrier, inc=1, device_id={"sub": high_peer(k)}, device_id_type=MESH)
    for k in range(1, n_low):
        pl.semaphore_signal(barrier, inc=1, device_id={"sub": low_peer(k)}, device_id_type=MESH)
    for kg in range(1, n_grp):
        for kl in range(n_low):
            pl.semaphore_signal(
                barrier, inc=1, device_id={"grp": grp_peer(kg), "sub": low_peer(kl)}, device_id_type=MESH)
    expected = (n_high - 1) + (n_low - 1) + (n_grp - 1) * n_low
    for h in has:
        expected = expected + jnp.where(h, 1, 0)
    pl.semaphore_wait(barrier, expected)

    def high_copy(r, k, ref, slot):
        return pltpu.make_async_remote_copy(
            src_ref=ref.at[slot], dst_ref=ref.at[slot],
            send_sem=hi_send.at[r, k], recv_sem=hi_recv.at[r, k],
            device_id={"sub": high_peer(k)}, device_id_type=MESH)

    def setup_copy(sends, recvs, k, ref, slot):
        return pltpu.make_async_remote_copy(
            src_ref=ref.at[slot], dst_ref=ref.at[slot],
            send_sem=sends, recv_sem=recvs,
            device_id={"sub": low_peer(k)}, device_id_type=MESH)

    def part_copy(c, k):
        return pltpu.make_async_remote_copy(
            src_ref=part_out.at[c, lax.rem(low + k, n_low)], dst_ref=part_in.at[c, k],
            send_sem=lo_send.at[1 + c, k], recv_sem=lo_recv.at[1 + c, k],
            device_id={"sub": low_peer(k)}, device_id_type=MESH)

    def u_copy(c, kg, kl):
        return pltpu.make_async_remote_copy(
            src_ref=part_out.at[c, n_low], dst_ref=ubuf.at[c, kg, kl],
            send_sem=u_send.at[c, kg, kl], recv_sem=u_recv.at[c, kg, kl],
            device_id={"grp": grp_peer(kg), "sub": low_peer(kl)}, device_id_type=MESH)

    def from_high(k):
        return lax.rem(high + n_high - k, n_high)

    def from_low(k):
        return lax.rem(low + n_low - k, n_low)

    def face_copy(r, f):
        return pltpu.make_async_remote_copy(
            src_ref=sendb.at[r, f], dst_ref=recvb.at[r, f ^ 1],
            send_sem=face_send.at[r, f], recv_sem=face_recv.at[r, f ^ 1],
            device_id=ids[f], device_id_type=MESH)

    def face_wait(r, f):
        pltpu.make_async_remote_copy(
            src_ref=sendb.at[r, f], dst_ref=recvb.at[r, f],
            send_sem=face_send.at[r, f], recv_sem=face_recv.at[r, f],
            device_id=ids[f], device_id_type=MESH).wait_recv()

    def each_face(r, value):
        for axis, side in sequence:
            f = side if axis == "grp" else side + 2
            present = (jnp.where(side == 1, g < n_grp - 1, g > 0) if axis == "grp"
                       else jnp.where(side == 1, j < n_sub - 1, j > 0))
            position = (g if axis == "grp" else j) + 2 * side - 1
            rows = pl.ds(pl.multiple_of(f * face, 16), face)
            sendb[r, f] = value(f, rows, jnp.where(present, 0.5, 1.0).astype(F32))

            @pl.when(present)
            def _():
                pltpu.make_async_remote_copy(
                    src_ref=sendb.at[r, f], dst_ref=recvb.at[r, f + 1 - 2 * side],
                    send_sem=face_send.at[r, f], recv_sem=face_recv.at[r, f + 1 - 2 * side],
                    device_id={axis: position}, device_id_type=MESH).start()

    def halves(out):
        return out[:, :columns] + out[:, columns:]

    def receive_face(r, f):
        @pl.when(has[f])
        def _():
            face_wait(r, f)
            sendb_rows = sendb[r, f] + recvb[r, f]
            direct[f] = sendb_rows

        @pl.when(jnp.logical_not(has[f]))
        def _():
            direct[f] = sendb[r, f]

    direct = recvb.at[1 + 2 * ITERS]

    def to_local(total):
        def chunk(i, carry):
            rows = pl.ds(pl.multiple_of(i * face, face), face)
            second = pl.ds(pl.multiple_of(order + i * face, face), face)
            out = dot(perm_t[rows, :], x2[...])
            xl2[rows, :] = out.astype(BF16)
            xl2[second, :] = out.astype(BF16)
            if total is not None:
                total[rows, :] += out[:, :columns] + out[:, columns:]
            return carry
        lax.fori_loop(0, 4, chunk, 0)

    def apply(matrix):
        def chunk(i, carry):
            rows = pl.ds(pl.multiple_of(i * face, face), face)
            out = dot(matrix[rows, :], xl2[...])
            upper, lower = split(out[:, :columns] + out[:, columns:])
            zx2[rows, :columns] = upper
            zx2[rows, columns:] = lower
            return carry
        lax.fori_loop(0, 4, chunk, 0)

    own_modes = jnp.concatenate([gm[...], jnp.zeros((modes, columns - modes), F32)], axis=1)
    line_modes[high] = own_modes
    peer_modes[low] = own_modes
    peer_rows[low] = ginv[...]
    for k in range(1, n_high):
        high_copy(0, k, line_modes, high).start()
    for k in range(1, n_low):
        setup_copy(lo_send.at[0, k], lo_recv.at[0, k], k, peer_modes, low).start()
        setup_copy(k_send.at[k], k_recv.at[k], k, peer_rows, low).start()

    map_row = fmap[...]
    tile = 128

    def build_t(i, carry):
        rows = pl.ds(pl.multiple_of(i * tile, tile), tile)
        local = lax.broadcasted_iota(jnp.int32, (tile, order), 0) + i * tile
        perm_t[rows, :] = jnp.where(local == map_row, 1.0, 0.0).astype(BF16)
        return carry
    lax.fori_loop(0, order // tile, build_t, 0)
    map_column = jnp.broadcast_to(map_row.astype(F32), (tile, order)).T
    lanes = lax.broadcasted_iota(jnp.int32, (order, tile), 1).astype(F32)
    for t in range(order // tile):
        perm[:, t * tile:(t + 1) * tile] = jnp.where(
            map_column == lanes + float(t * tile), 1.0, 0.0).astype(BF16)

    def split_load(i, carry):
        rows = pl.ds(pl.multiple_of(i * face, face), face)
        upper, lower = split(load[rows, :])
        zx2[rows, :columns] = upper
        zx2[rows, columns:] = lower
        return carry
    lax.fori_loop(0, 4, split_load, 0)
    each_face(0, lambda f, rows, w: halves(dot(perm[rows, :order], zx2[:order, :])))

    upper, lower = split(basis[...])
    moved = dot(jnp.concatenate([upper, lower], axis=0), perm_t[...])
    b2[...] = moved.astype(BF16)
    tail = perm.shape[1] - order
    padded = jnp.concatenate([moved, jnp.zeros((tail - 2 * modes, order), F32)], axis=0)
    perm[:, order:] = padded.T.astype(BF16)
    zx2[order:, :] = jnp.zeros((tail, 2 * columns), BF16)

    def permute_schur(start, stop):
        def chunk(i, carry):
            rows = pl.ds(pl.multiple_of(lax.rem(i, 4) * face, 16), face)
            lanes = pl.ds(pl.multiple_of(i // 4 * 2 * tile, 2 * tile), 2 * tile)
            sp2[rows, lanes] = dot(perm[rows, :order], s2[:, lanes]).astype(BF16)
            return carry
        lax.fori_loop(4 * start, 4 * stop, chunk, 0)
    blocks = order // tile

    def split_matrix(stage, matrix):
        def chunk(i, carry):
            rows = pl.ds(pl.multiple_of(i * tile, tile), tile)
            upper, lower = split(stage[rows, :])
            matrix[rows, :order] = upper
            matrix[rows, order:] = lower
            return carry
        lax.fori_loop(0, order // tile, chunk, 0)

    load_a.wait()
    split_matrix(stage_a, a2)
    load_s.wait()
    split_matrix(stage_s, s2)
    for k in range(1, n_high):
        high_copy(0, k, line_modes, from_high(k)).wait_recv()
    for k in range(1, n_low):
        setup_copy(lo_send.at[0, k], lo_recv.at[0, k], k, peer_modes, from_low(k)).wait_recv()
        setup_copy(k_send.at[k], k_recv.at[k], k, peer_rows, from_low(k)).wait_recv()
    line_t = line_modes[...].reshape(n_high * modes, columns).T[:modes, :]
    top_rows = top[pl.ds(pl.multiple_of(g * modes, modes), modes), :]
    top_in[...] = jnp.zeros_like(top_in)
    own_top = pl.ds(pl.multiple_of(g * modes, modes), modes)
    top_in[own_top, :n_high * modes] = line_t
    lane = lax.broadcasted_iota(jnp.int32, (n_sub * modes, n_high * modes), 1)
    target = lane + low * modes
    for k in range(1, n_high):
        target = target + jnp.where(lane >= k * modes, (n_low - 1) * modes, 0)
    row = lax.broadcasted_iota(jnp.int32, (n_sub * modes, n_high * modes), 0)
    chosen = jnp.where(row == target, 1.0, 0.0).astype(F32)
    own_part = exact_dot(peer_rows[...].reshape(n_low * modes, n_sub * modes), chosen)
    through = exact_dot(top_rows, top_in[:, :n_high * modes])
    peers = peer_modes[...].reshape(n_low * modes, columns)[:, :modes]
    rq[:n_low * modes, :] = own_part + exact_dot(peers, through)
    rq[n_low * modes:, :] = line_t
    nmat[...] = exact_dot(gm[...], top_rows)
    top_in[...] = jnp.zeros_like(top_in)
    permute_schur(0, blocks // 3)

    for f in range(4):
        receive_face(0, f)
        residual[f] = direct[f]

    sol_out[...] = jnp.zeros((order, columns), F32)
    centre = jnp.full((1, columns), 0.5 * (spec[0] + spec[1]), F32)
    half_width = jnp.full((1, columns), 0.5 * (spec[1] - spec[0]), F32)

    def precondition(r, c):
        for f in range(4):
            rows = slice(f * face, (f + 1) * face)
            upper, lower = split(residual[f] * weight[f])
            x2[rows, :columns] = upper
            x2[rows, columns:] = lower
        products = dot(b2[...], x2[...])
        products = products[:, :columns] + products[:, columns:]
        line[c, high] = products[:modes, :] + products[modes:, :]
        for k in range(1, n_high):
            high_copy(1 + c, k, line.at[c], high).start()
        to_local(None)
        apply(a2)
        for k in range(1, n_high):
            high_copy(1 + c, k, line.at[c], from_high(k)).wait_recv()
        parts = exact_dot(rq[...], line[c].reshape(n_high * modes, columns))
        part_out[c] = parts.reshape(n_low + 1, modes, columns)
        for kg in range(1, n_grp):
            for kl in range(n_low):
                u_copy(c, kg, kl).start()
        for k in range(1, n_low):
            part_copy(c, k).start()

        def outward(i, carry):
            rows = pl.ds(pl.multiple_of(i * face, 16), face)
            sendb[r, i] = halves(dot(perm[rows, :order], zx2[:order, :]))
            return carry
        lax.fori_loop(0, 4, outward, 0)
        if c == 0:
            permute_schur(blocks // 3, blocks // 2 + 1)
        update = part_out[c, low]
        for k in range(1, n_low):
            part_copy(c, k).wait_recv()
            update = update + part_in[c, k]
        for kg in range(1, n_grp):
            total = None
            for kl in range(n_low):
                u_copy(c, kg, kl).wait_recv()
                total = ubuf[c, kg, kl] if total is None else total + ubuf[c, kg, kl]
            source = lax.rem(g + n_grp - kg, n_grp)
            top_in[pl.ds(pl.multiple_of(source * modes, modes), modes), :] = total
        update = update + exact_dot(nmat[...], top_in[...])
        upper, lower = split(update)
        for base in (order, order + modes):
            zx2[base:base + modes, :columns] = upper
            zx2[base:base + modes, columns:] = lower
        each_face(r, lambda f, rows, w: (sendb[r, f] + halves(dot(perm[rows, order:], zx2[order:, :]))) * w)
        if c == 0:
            permute_schur(blocks // 2 + 1, blocks)
        for f in range(4):
            receive_face(r, f)

    precondition(1, 0)
    for f in range(4):
        direction[f] = direct[f] / centre
    rho = half_width / centre
    for turn in range(ITERS):
        for f in range(4):
            rows = slice(f * face, (f + 1) * face)
            upper, lower = split(direction[f])
            x2[rows, :columns] = upper
            x2[rows, columns:] = lower
        to_local(sol_out)
        r = 2 + 2 * turn
        each_face(r, lambda f, rows, w: halves(dot(sp2[rows, :], xl2[...])))
        for f in range(4):
            receive_face(r, f)
            residual[f] = residual[f] - direct[f]
        if turn + 1 < ITERS:
            rho_next = 1.0 / (2.0 * centre / half_width - rho)
            precondition(r + 1, 1 + turn)
            for f in range(4):
                direction[f] = rho_next * rho * direction[f] + (2.0 * rho_next / half_width) * direct[f]
            rho = rho_next

    for f in range(4):
        rows = slice(f * face, (f + 1) * face)
        upper, lower = split(residual[f])
        x2[rows, :columns] = upper
        x2[rows, columns:] = lower

    def finish(i, carry):
        rows = pl.ds(pl.multiple_of(i * face, face), face)
        out = dot(perm_t[rows, :], x2[...])
        res_out[rows, :] = out[:, :columns] + out[:, columns:]
        return carry
    lax.fori_loop(0, 4, finish, 0)

    for r in range(1 + 2 * ITERS):
        for f in range(4):
            @pl.when(has[f])
            def _():
                face_copy(r, f).wait_send()
    for k in range(1, n_high):
        high_copy(0, k, line_modes, high).wait_send()
    for k in range(1, n_low):
        setup_copy(lo_send.at[0, k], lo_recv.at[0, k], k, peer_modes, low).wait_send()
        setup_copy(k_send.at[k], k_recv.at[k], k, peer_rows, low).wait_send()
    for c in range(ITERS):
        for k in range(1, n_high):
            high_copy(1 + c, k, line.at[c], high).wait_send()
        for k in range(1, n_low):
            part_copy(c, k).wait_send()
        for kg in range(1, n_grp):
            for kl in range(n_low):
                u_copy(c, kg, kl).wait_send()


def solution(mesh):
    n_grp, n_sub = mesh.shape["grp"], mesh.shape["sub"]
    n_low = 1
    while n_low * n_low < n_sub:
        n_low *= 2
    n_high = n_sub // n_low

    def step(load, schur, linv, basis, ginv, gm, top, fmap, spec):
        order, columns = load.shape
        modes = basis.shape[0]
        face = order // 4
        tail = -(-2 * modes // 128) * 128
        rounds = 1 + ITERS
        faces = 1 + 2 * ITERS
        vmem = pl.BlockSpec(memory_space=pltpu.VMEM)
        hbm = pl.BlockSpec(memory_space=pl.ANY)
        smem = pl.BlockSpec(memory_space=pltpu.SMEM)
        dma = pltpu.SemaphoreType.DMA
        field = jax.ShapeDtypeStruct((order, columns), F32)
        return pl.pallas_call(
            functools.partial(kernel, n_grp, n_sub, n_low),
            out_shape=(field, field),
            in_specs=[vmem, hbm, hbm, vmem, vmem, vmem, vmem, vmem, smem],
            out_specs=(vmem, vmem),
            scratch_shapes=[
                pltpu.VMEM((order, order), F32),
                pltpu.VMEM((order, order), F32),
                pltpu.VMEM((order, 2 * order), BF16),
                pltpu.VMEM((order, 2 * order), BF16),
                pltpu.VMEM((order, 2 * order), BF16),
                pltpu.VMEM((order, order + tail), BF16),
                pltpu.VMEM((order, order), BF16),
                pltpu.VMEM((2 * modes, order), BF16),
                pltpu.VMEM((order, 2 * columns), BF16),
                pltpu.VMEM((2 * order, 2 * columns), BF16),
                pltpu.VMEM((order + tail, 2 * columns), BF16),
                pltpu.VMEM((4, face, columns), F32),
                pltpu.VMEM((4, face, columns), F32),
                pltpu.VMEM((faces, 4, face, columns), F32),
                pltpu.VMEM((faces + 1, 4, face, columns), F32),
                pltpu.VMEM((n_high, modes, columns), F32),
                pltpu.VMEM((n_low, modes, columns), F32),
                pltpu.VMEM((n_low, modes, n_sub * modes), F32),
                pltpu.VMEM((ITERS, n_high, modes, columns), F32),
                pltpu.VMEM((ITERS, n_low + 1, modes, columns), F32),
                pltpu.VMEM((ITERS, n_low, modes, columns), F32),
                pltpu.VMEM((ITERS, n_grp, n_low, modes, columns), F32),
                pltpu.VMEM((n_grp * modes, columns), F32),
                pltpu.VMEM(((n_low + 1) * modes, n_high * modes), F32),
                pltpu.VMEM((modes, n_grp * modes), F32),
                dma((2,)),
                dma((faces, 4)),
                dma((faces, 4)),
                dma((rounds, n_high)),
                dma((rounds, n_high)),
                dma((rounds, n_low)),
                dma((rounds, n_low)),
                dma((n_low,)),
                dma((n_low,)),
                dma((ITERS, n_grp, n_low)),
                dma((ITERS, n_grp, n_low)),
            ],
            compiler_params=pltpu.CompilerParams(
                collective_id=0, has_side_effects=True, vmem_limit_bytes=60 * 1024 * 1024
            ),
        )(load, schur, linv, basis, ginv, gm, top, fmap, spec)

    row = P(("grp", "sub"), None)
    return jax.shard_map(
        step,
        mesh=mesh,
        in_specs=(row, row, row, row, row, row, P(), row, P()),
        out_specs=(row, row),
        check_vma=False,
    )
```

```python
import functools

import jax
import jax.numpy as jnp
from jax import lax
from jax.experimental import pallas as pl
from jax.experimental.pallas import tpu as pltpu
from jax.sharding import PartitionSpec as P

ITERS = 3
F32 = jnp.float32
BF16 = jnp.bfloat16
MESH = pl.DeviceIdType.MESH


def dot(a, b):
    return jnp.dot(a, b, preferred_element_type=F32)


def exact_dot(a, b):
    return jnp.dot(a, b, precision=lax.Precision.HIGHEST, preferred_element_type=F32)


def split(v):
    high = v.astype(BF16)
    low = (v - high.astype(F32)).astype(BF16)
    return high, low


def kernel(
    n_grp, n_sub, n_low,
    load, schur, linv, basis, ginv, gm, top, fmap, spec,
    sol_out, res_out,
    stage_a, stage_s, a2, s2, sp2, perm, perm_t, b2, x2, xl2, zx2, direction, residual,
    sendb, recvb, line_modes, peer_modes, peer_rows, line, part_out, part_in, ubuf, top_in, rq, nmat,
    load_sem, face_send, face_recv, hi_send, hi_recv, lo_send, lo_recv, k_send, k_recv, u_send, u_recv,
):
    order, columns = load.shape
    face = order // 4
    modes = basis.shape[0]
    n_high = n_sub // n_low
    g = lax.axis_index("grp")
    j = lax.axis_index("sub")
    high, low = j // n_low, j % n_low
    has = [g > 0, g < n_grp - 1, j > 0, j < n_sub - 1]
    ids = [{"grp": g - 1}, {"grp": g + 1}, {"sub": j - 1}, {"sub": j + 1}]
    first = jnp.where(g == 0, 1, 0)
    third = jnp.where(j == 0, 1, 0)
    sequence = [("grp", first), ("grp", 1 - first), ("sub", third), ("sub", 1 - third)]
    weight = [jnp.where(h, 0.5, 1.0).astype(F32) for h in has]

    load_a = pltpu.make_async_copy(linv, stage_a, load_sem.at[0])
    load_s = pltpu.make_async_copy(schur, stage_s, load_sem.at[1])
    load_a.start()
    load_s.start()

    def high_peer(k):
        return lax.rem(high + k, n_high) * n_low + low

    def low_peer(k):
        return high * n_low + lax.rem(low + k, n_low)

    def grp_peer(k):
        return lax.rem(g + k, n_grp)

    barrier = pltpu.get_barrier_semaphore()
    for f in range(4):
        @pl.when(has[f])
        def _():
            pl.semaphore_signal(barrier, inc=1, device_id=ids[f], device_id_type=MESH)
    for k in range(1, n_high):
        pl.semaphore_signal(barrier, inc=1, device_id={"sub": high_peer(k)}, device_id_type=MESH)
    for k in range(1, n_low):
        pl.semaphore_signal(barrier, inc=1, device_id={"sub": low_peer(k)}, device_id_type=MESH)
    for kg in range(1, n_grp):
        for kl in range(n_low):
            pl.semaphore_signal(
                barrier, inc=1, device_id={"grp": grp_peer(kg), "sub": low_peer(kl)}, device_id_type=MESH)
    expected = (n_high - 1) + (n_low - 1) + (n_grp - 1) * n_low
    for h in has:
        expected = expected + jnp.where(h, 1, 0)
    pl.semaphore_wait(barrier, expected)

    def high_copy(r, k, ref, slot):
        return pltpu.make_async_remote_copy(
            src_ref=ref.at[slot], dst_ref=ref.at[slot],
            send_sem=hi_send.at[r, k], recv_sem=hi_recv.at[r, k],
            device_id={"sub": high_peer(k)}, device_id_type=MESH)

    def setup_copy(sends, recvs, k, ref, slot):
        return pltpu.make_async_remote_copy(
            src_ref=ref.at[slot], dst_ref=ref.at[slot],
            send_sem=sends, recv_sem=recvs,
            device_id={"sub": low_peer(k)}, device_id_type=MESH)

    def part_copy(c, k):
        return pltpu.make_async_remote_copy(
            src_ref=part_out.at[c, lax.rem(low + k, n_low)], dst_ref=part_in.at[c, k],
            send_sem=lo_send.at[1 + c, k], recv_sem=lo_recv.at[1 + c, k],
            device_id={"sub": low_peer(k)}, device_id_type=MESH)

    def u_copy(c, kg, kl):
        return pltpu.make_async_remote_copy(
            src_ref=part_out.at[c, n_low], dst_ref=ubuf.at[c, kg, kl],
            send_sem=u_send.at[c, kg, kl], recv_sem=u_recv.at[c, kg, kl],
            device_id={"grp": grp_peer(kg), "sub": low_peer(kl)}, device_id_type=MESH)

    def from_high(k):
        return lax.rem(high + n_high - k, n_high)

    def from_low(k):
        return lax.rem(low + n_low - k, n_low)

    def face_copy(r, f):
        return pltpu.make_async_remote_copy(
            src_ref=sendb.at[r, f], dst_ref=recvb.at[r, f ^ 1],
            send_sem=face_send.at[r, f], recv_sem=face_recv.at[r, f ^ 1],
            device_id=ids[f], device_id_type=MESH)

    def face_wait(r, f):
        pltpu.make_async_remote_copy(
            src_ref=sendb.at[r, f], dst_ref=recvb.at[r, f],
            send_sem=face_send.at[r, f], recv_sem=face_recv.at[r, f],
            device_id=ids[f], device_id_type=MESH).wait_recv()

    def each_face(r, value):
        for axis, side in sequence:
            f = side if axis == "grp" else side + 2
            present = (jnp.where(side == 1, g < n_grp - 1, g > 0) if axis == "grp"
                       else jnp.where(side == 1, j < n_sub - 1, j > 0))
            position = (g if axis == "grp" else j) + 2 * side - 1
            rows = pl.ds(pl.multiple_of(f * face, 16), face)
            sendb[r, f] = value(f, rows, jnp.where(present, 0.5, 1.0).astype(F32))

            @pl.when(present)
            def _():
                pltpu.make_async_remote_copy(
                    src_ref=sendb.at[r, f], dst_ref=recvb.at[r, f + 1 - 2 * side],
                    send_sem=face_send.at[r, f], recv_sem=face_recv.at[r, f + 1 - 2 * side],
                    device_id={axis: position}, device_id_type=MESH).start()

    def halves(out):
        return out[:, :columns] + out[:, columns:]

    def receive_face(r, f):
        @pl.when(has[f])
        def _():
            face_wait(r, f)
            sendb_rows = sendb[r, f] + recvb[r, f]
            direct[f] = sendb_rows

        @pl.when(jnp.logical_not(has[f]))
        def _():
            direct[f] = sendb[r, f]

    direct = recvb.at[1 + 2 * ITERS]

    def to_local(total):
        def chunk(i, carry):
            rows = pl.ds(pl.multiple_of(i * face, face), face)
            second = pl.ds(pl.multiple_of(order + i * face, face), face)
            out = dot(perm_t[rows, :], x2[...])
            xl2[rows, :] = out.astype(BF16)
            xl2[second, :] = out.astype(BF16)
            if total is not None:
                total[rows, :] += out[:, :columns] + out[:, columns:]
            return carry
        lax.fori_loop(0, 4, chunk, 0)

    def apply(matrix):
        def chunk(i, carry):
            rows = pl.ds(pl.multiple_of(i * face, face), face)
            out = dot(matrix[rows, :], xl2[...])
            upper, lower = split(out[:, :columns] + out[:, columns:])
            zx2[rows, :columns] = upper
            zx2[rows, columns:] = lower
            return carry
        lax.fori_loop(0, 4, chunk, 0)

    own_modes = jnp.concatenate([gm[...], jnp.zeros((modes, columns - modes), F32)], axis=1)
    line_modes[high] = own_modes
    peer_modes[low] = own_modes
    peer_rows[low] = ginv[...]
    for k in range(1, n_high):
        high_copy(0, k, line_modes, high).start()
    for k in range(1, n_low):
        setup_copy(lo_send.at[0, k], lo_recv.at[0, k], k, peer_modes, low).start()
        setup_copy(k_send.at[k], k_recv.at[k], k, peer_rows, low).start()

    map_row = fmap[...]
    tile = 128

    def build_t(i, carry):
        rows = pl.ds(pl.multiple_of(i * tile, tile), tile)
        local = lax.broadcasted_iota(jnp.int32, (tile, order), 0) + i * tile
        perm_t[rows, :] = jnp.where(local == map_row, 1.0, 0.0).astype(BF16)
        return carry
    lax.fori_loop(0, order // tile, build_t, 0)
    map_column = jnp.broadcast_to(map_row.astype(F32), (tile, order)).T
    lanes = lax.broadcasted_iota(jnp.int32, (order, tile), 1).astype(F32)
    for t in range(order // tile):
        perm[:, t * tile:(t + 1) * tile] = jnp.where(
            map_column == lanes + float(t * tile), 1.0, 0.0).astype(BF16)

    def split_load(i, carry):
        rows = pl.ds(pl.multiple_of(i * face, face), face)
        upper, lower = split(load[rows, :])
        zx2[rows, :columns] = upper
        zx2[rows, columns:] = lower
        return carry
    lax.fori_loop(0, 4, split_load, 0)
    each_face(0, lambda f, rows, w: halves(dot(perm[rows, :order], zx2[:order, :])))

    upper, lower = split(basis[...])
    moved = dot(jnp.concatenate([upper, lower], axis=0), perm_t[...])
    b2[...] = moved.astype(BF16)
    tail = perm.shape[1] - order
    padded = jnp.concatenate([moved, jnp.zeros((tail - 2 * modes, order), F32)], axis=0)
    perm[:, order:] = padded.T.astype(BF16)
    zx2[order:, :] = jnp.zeros((tail, 2 * columns), BF16)

    def permute_schur(start, stop):
        def chunk(i, carry):
            rows = pl.ds(pl.multiple_of(lax.rem(i, 4) * face, 16), face)
            lanes = pl.ds(pl.multiple_of(i // 4 * 2 * tile, 2 * tile), 2 * tile)
            sp2[rows, lanes] = dot(perm[rows, :order], s2[:, lanes]).astype(BF16)
            return carry
        lax.fori_loop(4 * start, 4 * stop, chunk, 0)
    blocks = order // tile

    def split_matrix(stage, matrix):
        def chunk(i, carry):
            rows = pl.ds(pl.multiple_of(i * tile, tile), tile)
            upper, lower = split(stage[rows, :])
            matrix[rows, :order] = upper
            matrix[rows, order:] = lower
            return carry
        lax.fori_loop(0, order // tile, chunk, 0)

    load_a.wait()
    split_matrix(stage_a, a2)
    load_s.wait()
    split_matrix(stage_s, s2)
    for k in range(1, n_high):
        high_copy(0, k, line_modes, from_high(k)).wait_recv()
    for k in range(1, n_low):
        setup_copy(lo_send.at[0, k], lo_recv.at[0, k], k, peer_modes, from_low(k)).wait_recv()
        setup_copy(k_send.at[k], k_recv.at[k], k, peer_rows, from_low(k)).wait_recv()
    line_t = line_modes[...].reshape(n_high * modes, columns).T[:modes, :]
    top_rows = top[pl.ds(pl.multiple_of(g * modes, modes), modes), :]
    top_in[...] = jnp.zeros_like(top_in)
    own_top = pl.ds(pl.multiple_of(g * modes, modes), modes)
    top_in[own_top, :n_high * modes] = line_t
    lane = lax.broadcasted_iota(jnp.int32, (n_sub * modes, n_high * modes), 1)
    target = lane + low * modes
    for k in range(1, n_high):
        target = target + jnp.where(lane >= k * modes, (n_low - 1) * modes, 0)
    row = lax.broadcasted_iota(jnp.int32, (n_sub * modes, n_high * modes), 0)
    chosen = jnp.where(row == target, 1.0, 0.0).astype(F32)
    own_part = exact_dot(peer_rows[...].reshape(n_low * modes, n_sub * modes), chosen)
    through = exact_dot(top_rows, top_in[:, :n_high * modes])
    peers = peer_modes[...].reshape(n_low * modes, columns)[:, :modes]
    rq[:n_low * modes, :] = own_part + exact_dot(peers, through)
    rq[n_low * modes:, :] = line_t
    nmat[...] = exact_dot(gm[...], top_rows)
    top_in[...] = jnp.zeros_like(top_in)
    permute_schur(0, blocks // 3)

    for f in range(4):
        receive_face(0, f)
        residual[f] = direct[f]

    sol_out[...] = jnp.zeros((order, columns), F32)
    centre = jnp.full((1, columns), 0.5 * (spec[0] + spec[1]), F32)
    half_width = jnp.full((1, columns), 0.5 * (spec[1] - spec[0]), F32)

    def precondition(r, c):
        for f in range(4):
            rows = slice(f * face, (f + 1) * face)
            upper, lower = split(residual[f] * weight[f])
            x2[rows, :columns] = upper
            x2[rows, columns:] = lower
        products = dot(b2[...], x2[...])
        products = products[:, :columns] + products[:, columns:]
        line[c, high] = products[:modes, :] + products[modes:, :]
        for k in range(1, n_high):
            high_copy(1 + c, k, line.at[c], high).start()
        to_local(None)
        apply(a2)
        for k in range(1, n_high):
            high_copy(1 + c, k, line.at[c], from_high(k)).wait_recv()
        parts = exact_dot(rq[...], line[c].reshape(n_high * modes, columns))
        part_out[c] = parts.reshape(n_low + 1, modes, columns)
        for kg in range(1, n_grp):
            for kl in range(n_low):
                u_copy(c, kg, kl).start()
        for k in range(1, n_low):
            part_copy(c, k).start()

        def outward(i, carry):
            rows = pl.ds(pl.multiple_of(i * face, 16), face)
            sendb[r, i] = halves(dot(perm[rows, :order], zx2[:order, :]))
            return carry
        lax.fori_loop(0, 4, outward, 0)
        if c == 0:
            permute_schur(blocks // 3, blocks // 2 + 1)
        update = part_out[c, low]
        for k in range(1, n_low):
            part_copy(c, k).wait_recv()
            update = update + part_in[c, k]
        for kg in range(1, n_grp):
            total = None
            for kl in range(n_low):
                u_copy(c, kg, kl).wait_recv()
                total = ubuf[c, kg, kl] if total is None else total + ubuf[c, kg, kl]
            source = lax.rem(g + n_grp - kg, n_grp)
            top_in[pl.ds(pl.multiple_of(source * modes, modes), modes), :] = total
        update = update + exact_dot(nmat[...], top_in[...])
        upper, lower = split(update)
        for base in (order, order + modes):
            zx2[base:base + modes, :columns] = upper
            zx2[base:base + modes, columns:] = lower
        each_face(r, lambda f, rows, w: (sendb[r, f] + halves(dot(perm[rows, order:], zx2[order:, :]))) * w)
        if c == 0:
            permute_schur(blocks // 2 + 1, blocks)
        for f in range(4):
            receive_face(r, f)

    precondition(1, 0)
    for f in range(4):
        direction[f] = direct[f] / centre
    rho = half_width / centre
    for turn in range(ITERS):
        for f in range(4):
            rows = slice(f * face, (f + 1) * face)
            upper, lower = split(direction[f])
            x2[rows, :columns] = upper
            x2[rows, columns:] = lower
        to_local(sol_out)
        r = 2 + 2 * turn
        each_face(r, lambda f, rows, w: halves(dot(sp2[rows, :], xl2[...])))
        for f in range(4):
            receive_face(r, f)
            residual[f] = residual[f] - direct[f]
        if turn + 1 < ITERS:
            rho_next = 1.0 / (2.0 * centre / half_width - rho)
            precondition(r + 1, 1 + turn)
            for f in range(4):
                direction[f] = rho_next * rho * direction[f] + (2.0 * rho_next / half_width) * direct[f]
            rho = rho_next

    for f in range(4):
        rows = slice(f * face, (f + 1) * face)
        upper, lower = split(residual[f])
        x2[rows, :columns] = upper
        x2[rows, columns:] = lower

    def finish(i, carry):
        rows = pl.ds(pl.multiple_of(i * face, face), face)
        out = dot(perm_t[rows, :], x2[...])
        res_out[rows, :] = out[:, :columns] + out[:, columns:]
        return carry
    lax.fori_loop(0, 4, finish, 0)

    for r in range(1 + 2 * ITERS):
        for f in range(4):
            @pl.when(has[f])
            def _():
                face_copy(r, f).wait_send()
    for k in range(1, n_high):
        high_copy(0, k, line_modes, high).wait_send()
    for k in range(1, n_low):
        setup_copy(lo_send.at[0, k], lo_recv.at[0, k], k, peer_modes, low).wait_send()
        setup_copy(k_send.at[k], k_recv.at[k], k, peer_rows, low).wait_send()
    for c in range(ITERS):
        for k in range(1, n_high):
            high_copy(1 + c, k, line.at[c], high).wait_send()
        for k in range(1, n_low):
            part_copy(c, k).wait_send()
        for kg in range(1, n_grp):
            for kl in range(n_low):
                u_copy(c, kg, kl).wait_send()


def hand_out(sol, res, sol_out, res_out):
    sol_out[...] = sol[...]
    res_out[...] = res[...]


def solution(mesh):
    n_grp, n_sub = mesh.shape["grp"], mesh.shape["sub"]
    n_low = 1
    while n_low * n_low < n_sub:
        n_low *= 2
    n_high = n_sub // n_low

    def step(load, schur, linv, basis, ginv, gm, top, fmap, spec):
        order, columns = load.shape
        modes = basis.shape[0]
        face = order // 4
        tail = -(-2 * modes // 128) * 128
        rounds = 1 + ITERS
        faces = 1 + 2 * ITERS
        vmem = pl.BlockSpec(memory_space=pltpu.VMEM)
        hbm = pl.BlockSpec(memory_space=pl.ANY)
        smem = pl.BlockSpec(memory_space=pltpu.SMEM)
        dma = pltpu.SemaphoreType.DMA
        field = jax.ShapeDtypeStruct((order, columns), F32)
        sol, res = pl.pallas_call(
            functools.partial(kernel, n_grp, n_sub, n_low),
            out_shape=(field, field),
            in_specs=[vmem, hbm, hbm, vmem, vmem, vmem, vmem, vmem, smem],
            out_specs=(vmem, vmem),
            scratch_shapes=[
                pltpu.VMEM((order, order), F32),
                pltpu.VMEM((order, order), F32),
                pltpu.VMEM((order, 2 * order), BF16),
                pltpu.VMEM((order, 2 * order), BF16),
                pltpu.VMEM((order, 2 * order), BF16),
                pltpu.VMEM((order, order + tail), BF16),
                pltpu.VMEM((order, order), BF16),
                pltpu.VMEM((2 * modes, order), BF16),
                pltpu.VMEM((order, 2 * columns), BF16),
                pltpu.VMEM((2 * order, 2 * columns), BF16),
                pltpu.VMEM((order + tail, 2 * columns), BF16),
                pltpu.VMEM((4, face, columns), F32),
                pltpu.VMEM((4, face, columns), F32),
                pltpu.VMEM((faces, 4, face, columns), F32),
                pltpu.VMEM((faces + 1, 4, face, columns), F32),
                pltpu.VMEM((n_high, modes, columns), F32),
                pltpu.VMEM((n_low, modes, columns), F32),
                pltpu.VMEM((n_low, modes, n_sub * modes), F32),
                pltpu.VMEM((ITERS, n_high, modes, columns), F32),
                pltpu.VMEM((ITERS, n_low + 1, modes, columns), F32),
                pltpu.VMEM((ITERS, n_low, modes, columns), F32),
                pltpu.VMEM((ITERS, n_grp, n_low, modes, columns), F32),
                pltpu.VMEM((n_grp * modes, columns), F32),
                pltpu.VMEM(((n_low + 1) * modes, n_high * modes), F32),
                pltpu.VMEM((modes, n_grp * modes), F32),
                dma((2,)),
                dma((faces, 4)),
                dma((faces, 4)),
                dma((rounds, n_high)),
                dma((rounds, n_high)),
                dma((rounds, n_low)),
                dma((rounds, n_low)),
                dma((n_low,)),
                dma((n_low,)),
                dma((ITERS, n_grp, n_low)),
                dma((ITERS, n_grp, n_low)),
            ],
            compiler_params=pltpu.CompilerParams(
                collective_id=0, has_side_effects=True, vmem_limit_bytes=60 * 1024 * 1024
            ),
        )(load, schur, linv, basis, ginv, gm, top, fmap, spec)
        return pl.pallas_call(
            hand_out, out_shape=(field, field), in_specs=[vmem, vmem], out_specs=(vmem, vmem)
        )(sol, res)

    row = P(("grp", "sub"), None)
    return jax.shard_map(
        step,
        mesh=mesh,
        in_specs=(row, row, row, row, row, row, P(), row, P()),
        out_specs=(row, row),
        check_vma=False,
    )
```
